32 devices in a mesh: pair: 8 (over z, x), pw: 4 (over y, core).
Axes of the slice: x: 2, y: 2, z: 4, core: 2. Of those that a mesh axis runs over, the one named last changes fastest.
Arguments:
- pair_matrix: bfloat16 [384, 12288], P('pair', 'pw'), may hold values from -6 to 6
- basis: bfloat16 [12288, 768], P('pw'), may hold values from -0.078125 to 0.078125
- valence: int32 [384], P('pair'), may hold values from 0 to 127
- conduction: int32 [384], P('pair'), may hold values from 64 to 255
- occupation: int32 [256], replicated, may hold values from 0 to 2
- energy: int32 [256], replicated, may hold values from 0 to 999
Outputs:
- chi: float32 [2, 768, 768], P(None, 'pair', 'pw')
The draws below stay inside these ranges and needn't reach their ends.
All inputs are finite; a program needn't handle non-finite values.
Results may differ from the reference program's by a relative error of at most 0.005.
Values may be sent and summed in bfloat16 or wider, within the bound.
No kernel may reach another device: no remote copies, remote signals or barrier semaphores. Data moves between devices by JAX's collectives and lax.ppermute only.
A program may use at most 64 MiB of HBM per device.

```python
import jax
import jax.numpy as jnp
from jax import lax

NB = 768
G = 12288
BANDS = 256
W = 2
PAIRS = 384


def with_ends(drawn, own_key, low, top_value):
    place = [jax.random.randint(jax.random.fold_in(own_key, axis), (), 0, length) for axis, length in enumerate(drawn.shape)]
    widest = drawn.shape.index(max(drawn.shape))
    beside = place[:widest] + [(place[widest] + 1) % drawn.shape[widest]] + place[widest + 1:]
    return drawn.at[tuple(place)].set(low).at[tuple(beside)].set(top_value)


def with_spikes(values, stream_key, source, target, parts, factor):
    def block_of(position):
        return (jnp.arange(values.shape[position]) // (values.shape[position] // parts)).reshape((-1,) + (1,) * (values.ndim - 1 - position))

    one_side = jax.random.permutation(stream_key, parts)[block_of(target)]
    other_side = (block_of(target) + parts // 2) % parts
    return jnp.where((block_of(source) == one_side) | (block_of(source) == other_side), factor * values, values)


def levels(stream_key, extent, cuts, smallest, largest):
    loudness, own = 1.0, jax.random.fold_in(stream_key, 6)
    for axis_at, blocks in cuts:
        draws = jnp.exp(jax.random.uniform(jax.random.fold_in(own, axis_at), (blocks,), jnp.float32, smallest / len(cuts), largest / len(cuts)))
        loudness = loudness * jnp.repeat(draws, extent[axis_at] // blocks).reshape([-1 if axis == axis_at else 1 for axis in range(len(extent))])
    return loudness


def noise(stream_key, extent, scale, most, cuts=(), dtype=jnp.bfloat16):
    entries = jax.random.normal(stream_key, extent, jnp.float32) * scale
    if len(cuts) > 0:
        entries = levels(stream_key, extent, cuts, -0.22, 0.18) * entries
    return jnp.clip(entries, min=-most, max=most).astype(dtype)


def gaussian_with(rng, dims, scale, bound, cuts, heavy, kind=jnp.bfloat16):
    values = scale * jax.random.normal(rng, dims, jnp.float32)
    if cuts:
        values = values * levels(rng, dims, cuts, -0.22, 0.18)
    return jnp.clip(with_spikes(values, jax.random.fold_in(rng, 3), *heavy), -bound, bound).astype(kind)


def setup_inputs(seed: int = 0) -> dict:
    key_of = jax.random.split(jax.random.key(seed), 7)
    pair_matrix = noise(key_of[0], (PAIRS, G), 1.0, 6.0, ((0, 8), (1, 4)))
    basis = gaussian_with(key_of[1], (G, NB), G ** -0.5, 0.078125, ((0, 4),), (0, 1, 4, 2.0))
    valence = with_ends(jax.random.randint(key_of[2], (PAIRS,), 0, BANDS // 2), jax.random.fold_in(key_of[2], 1), 0, (BANDS // 2) - 1).astype(jnp.int32)
    conduction = with_ends(jax.random.randint(key_of[3], (PAIRS,), BANDS // 4, BANDS), jax.random.fold_in(key_of[3], 1), BANDS // 4, BANDS - 1).astype(jnp.int32)
    occupation = with_ends(jax.random.randint(key_of[4], (BANDS,), 0, 3), jax.random.fold_in(key_of[4], 1), 0, 2).astype(jnp.int32)
    energy = with_ends(jax.random.randint(key_of[5], (BANDS,), 0, 1000), jax.random.fold_in(key_of[5], 1), 0, 999).astype(jnp.int32)
    return dict(pair_matrix=pair_matrix, basis=basis, valence=valence, conduction=conduction, occupation=occupation, energy=energy)


def reference(pair_matrix, basis, valence, conduction, occupation, energy):
    projection = jnp.dot(pair_matrix, basis, preferred_element_type=jnp.float32).astype(jnp.bfloat16)
    gap = (energy[conduction] - energy[valence]).astype(jnp.float32) * 0.01
    filling = (occupation[valence] - occupation[conduction]).astype(jnp.float32)
    freq = 0.5 * (jnp.arange(W).astype(jnp.float32) + 1.0)
    weights = filling[None, :] * 2.0 * gap[None, :] / (freq[:, None] ** 2 + gap[None, :] ** 2)
    weights = weights / jnp.sqrt(jnp.float32(PAIRS))

    def one_freq(weight_row):
        scaled = (weight_row[:, None] * projection.astype(jnp.float32)).astype(jnp.bfloat16)
        return jnp.dot(scaled.T, projection, preferred_element_type=jnp.float32)
    return lax.map(one_freq, weights)
```

```python
import jax
import jax.numpy as jnp
from jax import lax
from jax.sharding import PartitionSpec as P

W = 2


def lookup(index, table):
    bands = table.shape[0]
    match = index[:, None] == jnp.arange(bands)[None, :]
    return jnp.sum(jnp.where(match, table[None, :], 0), axis=1)


def three_parts(w):
    parts = []
    for _ in range(3):
        top = lax.reduce_precision(w, 8, 7)
        parts.append(top.astype(jnp.bfloat16))
        w = w - top
    return parts


def shards(pair_matrix, basis, valence, conduction, occupation, energy):
    rows = pair_matrix.shape[0]
    modes = basis.shape[1]
    n_pair, n_pw = lax.axis_size("pair"), lax.axis_size("pw")
    a_cols, b_cols, half = modes // n_pair, modes // n_pw, modes // 2
    me_pw = lax.axis_index("pw")

    gap = (lookup(conduction, energy) - lookup(valence, energy)).astype(jnp.float32) * 0.01
    filling = (lookup(valence, occupation) - lookup(conduction, occupation)).astype(jnp.float32)
    freq = 0.5 * (jnp.arange(W).astype(jnp.float32) + 1.0)
    weights = filling[None, :] * 2.0 * gap[None, :] / (freq[:, None] ** 2 + gap[None, :] ** 2)
    weights = weights / jnp.sqrt(jnp.float32(rows * n_pair))
    weight_cols = jnp.stack(three_parts(weights), 0).reshape(3 * W, rows).T

    def swap(x, bit):
        return lax.ppermute(x, "pw", [(j, j ^ bit) for j in range(n_pw)])

    partial = jnp.dot(pair_matrix, basis, preferred_element_type=jnp.float32)
    low, high = partial[:, :half], partial[:, half:]
    odd = me_pw % 2 == 1
    mine = jnp.where(odd, high, low)
    mine = mine + swap(jnp.where(odd, low, high), 1)
    bit = 2
    while bit < n_pw:
        mine = mine + swap(mine, bit)
        bit *= 2
    mine = mine.astype(jnp.bfloat16)
    other = swap(mine, 1)
    proj = jnp.concatenate([jnp.where(odd, other, mine), jnp.where(odd, mine, other)], axis=1)

    left = proj.reshape(rows, n_pair, a_cols).transpose(1, 0, 2)
    right = lax.dynamic_slice_in_dim(proj, me_pw * b_cols, b_cols, axis=1)
    tail = jnp.concatenate([right, weight_cols], axis=1)
    message = jnp.concatenate(
        [left, jnp.broadcast_to(tail[None], (n_pair,) + tail.shape)], axis=2
    )
    message = lax.all_to_all(message, "pair", 0, 0, tiled=True).reshape(n_pair * rows, -1)

    left, right = message[:, :a_cols], message[:, a_cols : a_cols + b_cols]
    w = message[:, a_cols + b_cols :].astype(jnp.float32).reshape(-1, 3, W).sum(axis=1)
    scaled = (w[:, :, None] * left.astype(jnp.float32)[:, None, :]).astype(jnp.bfloat16)
    return jnp.einsum("pka,pb->kab", scaled, right, preferred_element_type=jnp.float32)


def solution(mesh):
    return jax.shard_map(
        shards,
        mesh=mesh,
        in_specs=(P("pair", "pw"), P("pw", None), P("pair"), P("pair"), P(), P()),
        out_specs=P(None, "pair", "pw"),
        check_vma=False,
    )
```
